256 devices in a mesh: ka: 32 (over z_hi, y, core), pa: 8 (over z_lo, x).
Axes of the slice: x: 4, y: 4, z: 8 (z_hi: 4, z_lo: 2; z = z_hi * 2 + z_lo), core: 2. Of those that a mesh axis runs over, the one named last changes fastest.
Arguments:
- orbitals: bfloat16 [32, 4096, 128], P('ka', 'pa'), may hold values from -0.75 to 0.75
- occupied: int32 [32], P('ka'), may hold values from 32 to 64
- plus_partner: int32 [32], P('ka'), may hold values from 0 to 31, as said below
- minus_partner: int32 [32], P('ka'), may hold values from 0 to 31, as said below
- coulomb: bfloat16 [2, 4096, 4096], P(None, 'pa'), as said below
Outputs:
- exchange_out: float32 [32, 4096, 128], P('ka', 'pa')
The draws below stay inside these ranges and needn't reach their ends.
Inputs may be any that keep to these rules, and one draw needn't show every extreme that they name: `plus_partner`: a permutation of the 32 window positions. `minus_partner`: the inverse permutation of plus_partner. `coulomb`: each of the two kernels is a symmetric matrix.
All inputs are finite; a program needn't handle non-finite values.
Results may differ from the reference program's by a relative error of at most 0.0003.
Values may be sent and summed in bfloat16 or wider, within the bound.
A program may use at most 128 MiB of HBM per device.

```python
import math
import jax
import jax.numpy as jnp
from jax import lax

NB = 64
NMU = 4096
KPTS = 32


def partner_order(key):
    return jax.random.permutation(jax.random.fold_in(key, 17), KPTS).astype(jnp.int32)


def draw_plus_partner(key, part):
    return partner_order(key)


def draw_minus_partner(key, part):
    order = partner_order(key)
    return jnp.argsort(order, stable=True).astype(jnp.int32)


def draw_coulomb(key, part):
    subkeys = jax.random.split(jax.random.fold_in(key, 29), 2)
    normal_part = jnp.clip(jax.random.normal(subkeys[0], (2, NMU, NMU), jnp.float32), -4.0, 4.0)
    symmetric = (normal_part + jnp.swapaxes(normal_part, 1, 2)) * (0.3 / math.sqrt(2.0))
    diagonal = jnp.exp(jax.random.uniform(subkeys[1], (2, NMU), jnp.float32, math.log(0.5), math.log(2.0)))
    kernel = symmetric + diagonal[:, :, None] * jnp.eye(NMU, dtype=jnp.float32)[None]
    return kernel.astype(jnp.bfloat16)


def set_ends(array, rng, smallest, largest):
    place = [jax.random.randint(jax.random.fold_in(rng, axis), (), 0, length) for axis, length in enumerate(array.shape)]
    main_axis = array.shape.index(max(array.shape))
    neighbour = place[:main_axis] + [(place[main_axis] + 1) % array.shape[main_axis]] + place[main_axis + 1:]
    return array.at[tuple(place)].set(smallest).at[tuple(neighbour)].set(largest)


def levels(stream_key, dims, cuts, smallest, high):
    def one(dim, blocks):
        steps = jax.random.uniform(jax.random.fold_in(jax.random.fold_in(stream_key, 6), dim), (blocks,), jnp.float32, smallest / len(cuts), high / len(cuts))
        return jnp.repeat(jnp.exp(steps), dims[dim] // blocks).reshape((-1,) + (1,) * (len(dims) - dim - 1))

    loudness = one(*cuts[0])
    for cut in cuts[1:]:
        loudness = loudness * one(*cut)
    return loudness


def gaussian(own_key, extent, deviation, bound, cuts=(), kind=jnp.bfloat16):
    level = levels(own_key, extent, cuts, -0.22, 0.18) if cuts else 1.0
    result = jax.random.normal(own_key, extent, jnp.float32) * deviation * level
    return jnp.minimum(jnp.maximum(result, -bound), bound).astype(kind)


def setup_inputs(seed: int = 0) -> dict:
    arg_keys = jax.random.split(jax.random.key(seed), 6)
    return {
        "orbitals": gaussian(arg_keys[0], (KPTS, NMU, 2 * NB), 0.125, 0.75, ((0, 32), (1, 8))),
        "occupied": set_ends(jax.random.randint(arg_keys[1], (KPTS,), NB // 2, NB + 1), jax.random.fold_in(arg_keys[1], 1), NB // 2, NB).astype(jnp.int32),
        "plus_partner": draw_plus_partner(jax.random.fold_in(arg_keys[5], 71), 0),
        "minus_partner": draw_minus_partner(jax.random.fold_in(arg_keys[5], 71), 0),
        "coulomb": draw_coulomb(jax.random.fold_in(arg_keys[5], 71), 0),
    }


def rotate(block):
    bands = block.shape[-1] // 2
    return jnp.concatenate([block[..., bands:], -block[..., :bands]], axis=-1)


def reference(orbitals, occupied, plus_partner, minus_partner, coulomb):
    channels = orbitals.shape[2]
    bands = channels // 2
    band_index = jnp.arange(channels, dtype=jnp.int32) % bands
    keep_mask = band_index[None, None, :] < occupied[:, None, None]
    masked = jnp.where(keep_mask, orbitals, jnp.zeros_like(orbitals))
    row_block = math.gcd(NMU, 512)

    def one_kpoint(kpoint):
        upper_half = orbitals[kpoint].astype(jnp.float32)
        bottom = jnp.concatenate([-upper_half[:, bands:], upper_half[:, :bands]], axis=1)
        partners = (masked[plus_partner[kpoint]], masked[minus_partner[kpoint]])

        def one_block(row_start):
            mixed_real = jnp.zeros((row_block, NMU), jnp.float32)
            mixed_imag = jnp.zeros((row_block, NMU), jnp.float32)
            for partner in range(2):
                full_partner = partners[partner]
                row_part = lax.dynamic_slice_in_dim(full_partner, row_start, row_block, 0)
                real_part = jnp.dot(row_part, full_partner.T, preferred_element_type=jnp.float32)
                imag_part = jnp.dot(rotate(row_part), full_partner.T, preferred_element_type=jnp.float32)
                kernel_tile = lax.dynamic_slice_in_dim(coulomb[partner], row_start, row_block, 0).astype(jnp.float32)
                mixed_real = mixed_real + kernel_tile * real_part
                mixed_imag = mixed_imag + kernel_tile * imag_part
            applied = jnp.dot(mixed_real, upper_half, precision=lax.Precision.HIGHEST, preferred_element_type=jnp.float32)
            applied = applied + jnp.dot(mixed_imag, bottom, precision=lax.Precision.HIGHEST, preferred_element_type=jnp.float32)
            return -applied

        starts = jnp.arange(0, NMU, row_block, dtype=jnp.int32)
        return lax.map(one_block, starts).reshape(NMU, channels)

    return lax.map(one_kpoint, jnp.arange(KPTS, dtype=jnp.int32))
```

```python
import functools

import jax
import jax.numpy as jnp
from jax import lax
from jax.experimental import pallas as pl
from jax.experimental.pallas import tpu as pltpu
from jax.sharding import PartitionSpec as P

MESH = pl.DeviceIdType.MESH
PLUS, MINUS, OWN = 0, 1, 2
last_dims = (((1,), (1,)), ((), ()))
row_tile = 256


def kernel(
    ka, pa, orb, occ, plus, minus, coul, out,
    gath, first, ids_row, ids_all, ids_s, picked, cbuf, lhs,
    own_sem, coul_sem, ids_copy_sem, ids_send, ids_recv,
    first_send, first_recv, second_send, second_recv, gather_send, gather_recv,
):
    k, p = lax.axis_index("ka"), lax.axis_index("pa")
    xs = pa // 2
    z, x = p // xs, lax.rem(p, xs)
    other = 1 - z
    right, left, far = [lax.rem(x + step, xs) for step in (1, xs - 1, 2)]
    at = lambda plane, column: plane * xs + column
    half = ka // 2
    whole, low, high = pl.ds(0, ka), pl.ds(0, half), pl.ds(half, half)
    bands = out.shape[2] // 2

    own_copy = pltpu.make_async_copy(orb, gath.at[OWN, pl.ds(p, 1)], own_sem)
    own_copy.start()
    coul_copy = pltpu.make_async_copy(coul, cbuf, coul_sem)
    coul_copy.start()
    lane = lax.broadcasted_iota(jnp.int32, (1, 2 * bands), 1)
    ids_row[...] = jnp.where(lane == PLUS, plus[0], jnp.where(lane == MINUS, minus[0], occ[0]))

    barrier = pltpu.get_barrier_semaphore()

    def greet(step, carry):
        pl.semaphore_signal(barrier, inc=1, device_id=(lax.rem(k + step, ka), p), device_id_type=MESH)
        return carry

    lax.fori_loop(1, ka, greet, 0)
    for peer in (at(other, x), at(z, right), at(z, left)):
        pl.semaphore_signal(barrier, inc=1, device_id=(k, peer), device_id_type=MESH)
    own_copy.wait()
    pl.semaphore_wait(barrier, ka + 2)

    def to(source, target, send, recv, device):
        pltpu.make_async_remote_copy(
            src_ref=source, dst_ref=target, send_sem=send, recv_sem=recv,
            device_id=device, device_id_type=MESH,
        ).start()

    def arrived(ref, sem):
        pltpu.make_async_copy(ref, ref, sem).wait()

    def spread(step, carry):
        j = lax.rem(k + step, ka)
        to(ids_row, ids_all.at[k], ids_send, ids_recv, (j, p))
        to(gath.at[OWN, p, j], first.at[k], first_send, first_recv, (j, p))
        return carry

    pltpu.make_async_copy(ids_row, ids_all.at[k], ids_recv).start()
    pltpu.make_async_copy(gath.at[OWN, p, k], first.at[k], first_recv).start()
    lax.fori_loop(1, ka, spread, 0)

    def hop(item, slot, block, rows, peer):
        part = gath.at[item, block, rows]
        to(part, part, gather_send.at[item, slot], gather_recv.at[item, slot], (k, peer))

    def landed(item, slot, block, rows):
        arrived(gath.at[item, block, rows], gather_recv.at[item, slot])

    def stage_own(item):
        hop(item, 1, p, whole, at(z, right))
        hop(item, 2, p, whole, at(z, left))
        hop(item, 0, p, whole, at(other, x))

    def stage_pair(item):
        landed(item, 0, at(other, x), whole)
        hop(item, 3, at(other, x), whole, at(z, right))
        hop(item, 4, at(other, x), whole, at(z, left))

    def stage_far(item):
        landed(item, 1, at(z, left), whole)
        hop(item, 5, at(z, left), low, at(z, right))
        landed(item, 2, at(z, right), whole)
        hop(item, 6, at(z, right), high, at(z, left))

    def stage_cross(item):
        landed(item, 5, at(z, far), low)
        hop(item, 7, at(z, far), low, at(other, x))
        landed(item, 6, at(z, far), high)
        hop(item, 8, at(z, far), high, at(other, x))

    def sides(item):
        landed(item, 3, at(other, left), whole)
        landed(item, 4, at(other, right), whole)

    def last(item):
        landed(item, 7, at(other, far), low)
        landed(item, 8, at(other, far), high)

    stage_own(OWN)

    arrived(ids_all, ids_recv)
    ids_copy = pltpu.make_async_copy(ids_all, ids_s, ids_copy_sem)
    ids_copy.start()
    ids_copy.wait()
    arrived(first, first_recv)
    band = lax.rem(lax.broadcasted_iota(jnp.int32, first.shape[1:], 1), bands)

    for item in (PLUS, MINUS):
        def choose(j, carry):
            partner = ids_s[j, 0, item]
            piece = first[partner].astype(jnp.float32)
            keep = band < ids_s[partner, 0, 2]
            picked[item, j] = jnp.where(keep, piece, jnp.zeros_like(piece)).astype(jnp.bfloat16)
            return carry

        lax.fori_loop(0, ka, choose, 0)

        def deliver(step, carry):
            j = lax.rem(k + step, ka)
            to(picked.at[item, j], gath.at[item, p, k], second_send.at[item], second_recv.at[item], (j, p))
            return carry

        pltpu.make_async_copy(picked.at[item, k], gath.at[item, p, k], second_recv.at[item]).start()
        lax.fori_loop(1, ka, deliver, 0)

    stage_pair(OWN)
    stage_far(OWN)
    stage_cross(OWN)

    rows = ka * first.shape[1]
    for item in (PLUS, MINUS):
        arrived(gath.at[item, p], second_recv.at[item])
        stage_own(item)
        mine = gath[item, p].reshape(rows, 2 * bands)
        lhs[item, 0] = mine
        lhs[item, 1] = jnp.concatenate([mine[:, bands:], -mine[:, :bands]], axis=1)

    sides(OWN)
    last(OWN)
    coul_copy.wait()

    tile = min(row_tile, rows)

    def apply(block, fresh=False):
        start = pl.multiple_of(block * rows, rows)
        phi = gath[OWN, block].reshape(rows, 2 * bands)
        turned = jnp.concatenate([-phi[:, bands:], phi[:, :bands]], axis=1)
        others = [gath[item, block].reshape(rows, 2 * bands) for item in (PLUS, MINUS)]

        def one_tile(index, carry):
            here = pl.ds(pl.multiple_of(index * tile, tile), tile)
            kernels = [cbuf[item, here, pl.ds(start, rows)].astype(jnp.float32) for item in (PLUS, MINUS)]
            total = jnp.zeros((tile, 2 * bands), jnp.float32)
            for part, values in ((0, phi), (1, turned)):
                mixed = sum(
                    kernels[item]
                    * lax.dot_general(
                        lhs[item, part, here], others[item], last_dims, preferred_element_type=jnp.float32
                    )
                    for item in (PLUS, MINUS)
                )
                upper = mixed.astype(jnp.bfloat16)
                lower = (mixed - upper.astype(jnp.float32)).astype(jnp.bfloat16)
                total = total + jnp.dot(upper, values, preferred_element_type=jnp.float32)
                total = total + jnp.dot(lower, values, preferred_element_type=jnp.float32)
            if fresh:
                out[0, here] = -total
            else:
                out[0, here] = out[0, here] - total
            return carry

        lax.fori_loop(0, rows // tile, one_tile, 0)

    for item in (PLUS, MINUS):
        stage_pair(item)
    apply(p, fresh=True)
    for item in (PLUS, MINUS):
        stage_far(item)
    apply(at(other, x))
    apply(at(z, left))
    apply(at(z, right))
    for item in (PLUS, MINUS):
        stage_cross(item)
    apply(at(z, far))
    for item in (PLUS, MINUS):
        sides(item)
    apply(at(other, left))
    apply(at(other, right))
    for item in (PLUS, MINUS):
        last(item)
    apply(at(other, far))

    arrived(ids_all.at[pl.ds(0, ka - 1)], ids_send)
    arrived(first.at[pl.ds(0, ka - 1)], first_send)
    for item in (PLUS, MINUS):
        arrived(picked.at[item, pl.ds(0, ka - 1)], second_send.at[item])
    for item in (PLUS, MINUS, OWN):
        for slot in range(9):
            arrived(gath.at[item, 0, whole if slot < 5 else low], gather_send.at[item, slot])


def body(ka, pa, orbitals, occupied, plus_partner, minus_partner, coulomb):
    _, rows, channels = orbitals.shape
    piece = rows // ka
    dma = pltpu.SemaphoreType.DMA
    vmem = pl.BlockSpec(memory_space=pltpu.VMEM)
    smem = pl.BlockSpec(memory_space=pltpu.SMEM)
    hbm = pl.BlockSpec(memory_space=pl.ANY)
    return pl.pallas_call(
        functools.partial(kernel, ka, pa),
        out_shape=jax.ShapeDtypeStruct((1, rows, channels), jnp.float32),
        in_specs=[hbm, smem, smem, smem, hbm],
        out_specs=vmem,
        scratch_shapes=[
            pltpu.VMEM((3, pa, ka, piece, channels), jnp.bfloat16),
            pltpu.VMEM((ka, piece, channels), jnp.bfloat16),
            pltpu.VMEM((1, channels), jnp.int32),
            pltpu.VMEM((ka, 1, channels), jnp.int32),
            pltpu.SMEM((ka, 1, channels), jnp.int32),
            pltpu.VMEM((2, ka, piece, channels), jnp.bfloat16),
            pltpu.VMEM(coulomb.shape, jnp.bfloat16),
            pltpu.VMEM((2, 2, rows, channels), jnp.bfloat16),
            dma, dma, dma, dma, dma, dma, dma, dma((2,)), dma((2,)), dma((3, 9)), dma((3, 9)),
        ],
        compiler_params=pltpu.CompilerParams(collective_id=0, has_side_effects=True),
        name="exchange",
    )(orbitals.reshape(1, ka, piece, channels), occupied, plus_partner, minus_partner, coulomb)


def solution(mesh):
    placed = (P("ka", "pa", None), P("ka"), P("ka"), P("ka"), P(None, "pa", None))
    return jax.shard_map(
        functools.partial(body, mesh.shape["ka"], mesh.shape["pa"]),
        mesh=mesh, in_specs=placed, out_specs=P("ka", "pa", None), check_vma=False,
    )
```

```python
import functools

import jax
import jax.numpy as jnp
from jax import lax
from jax.experimental import pallas as pl
from jax.experimental.pallas import tpu as pltpu
from jax.sharding import PartitionSpec as P

MESH = pl.DeviceIdType.MESH
PLUS, MINUS, OWN = 0, 1, 2
last_dims = (((1,), (1,)), ((), ()))


def kernel(
    ka, pa, orb, occ, plus, minus, coul, out,
    gath, first, numbers, ids_row, ids_all, ids_s, picked, cbuf, lhs,
    own_sem, coul_sem, number_sems, ids_copy_sem, ids_send, ids_recv,
    first_send, first_recv, second_send, second_recv, gather_send, gather_recv,
):
    k, p = lax.axis_index("ka"), lax.axis_index("pa")
    xs = pa // 2
    z, x = p // xs, lax.rem(p, xs)
    other = 1 - z
    right, left, far = [lax.rem(x + step, xs) for step in (1, xs - 1, 2)]
    at = lambda plane, column: plane * xs + column
    half = ka // 2
    whole, low, high = (0, ka), (0, half), (half, half)
    bands = out.shape[2] // 2
    piece = first.shape[1]

    barrier = pltpu.get_barrier_semaphore()

    def greet(step, carry):
        pl.semaphore_signal(barrier, inc=1, device_id=(lax.rem(k + step, ka), p), device_id_type=MESH)
        return carry

    lax.fori_loop(1, ka, greet, 0)
    for peer in (at(other, x), at(z, right), at(z, left)):
        pl.semaphore_signal(barrier, inc=1, device_id=(k, peer), device_id_type=MESH)

    own_copy = pltpu.make_async_copy(orb, gath.at[OWN, pl.ds(p, 1)], own_sem)
    own_copy.start()
    number_copies = [
        pltpu.make_async_copy(ref, numbers.at[index], number_sems.at[index])
        for index, ref in enumerate((plus, minus, occ))
    ]
    for copy in number_copies:
        copy.start()
    coul_copy = pltpu.make_async_copy(coul, cbuf, coul_sem)
    coul_copy.start()
    for copy in number_copies:
        copy.wait()
    lane = lax.broadcasted_iota(jnp.int32, (1, 2 * bands), 1)
    ids_row[...] = jnp.where(lane == 0, numbers[0, 0], jnp.where(lane == 1, numbers[1, 0], numbers[2, 0]))
    own_copy.wait()
    pl.semaphore_wait(barrier, ka + 2)

    def to(source, target, send, recv, device):
        pltpu.make_async_remote_copy(
            src_ref=source, dst_ref=target, send_sem=send, recv_sem=recv,
            device_id=device, device_id_type=MESH,
        ).start()

    def arrived(ref, sem):
        pltpu.make_async_copy(ref, ref, sem).wait()

    def spread(step, carry):
        j = lax.rem(k + step, ka)
        to(ids_row, ids_all.at[k], ids_send, ids_recv, (j, p))
        to(gath.at[OWN, p, j], first.at[k], first_send, first_recv, (j, p))
        return carry

    pltpu.make_async_copy(ids_row, ids_all.at[k], ids_recv).start()
    pltpu.make_async_copy(gath.at[OWN, p, k], first.at[k], first_recv).start()
    lax.fori_loop(1, ka, spread, 0)

    def hop(item, slot, block, rows, peer):
        part = gath.at[item, block, pl.ds(*rows)]
        to(part, part, gather_send.at[item, slot], gather_recv.at[item, slot], (k, peer))

    def landed(item, slot, block, rows):
        arrived(gath.at[item, block, pl.ds(*rows)], gather_recv.at[item, slot])

    def send_own(item):
        hop(item, 1, p, whole, at(z, right))
        hop(item, 2, p, whole, at(z, left))
        hop(item, 0, p, whole, at(other, x))

    def send_far(item):
        landed(item, 1, at(z, left), whole)
        hop(item, 3, at(z, left), low, at(z, right))
        landed(item, 2, at(z, right), whole)
        hop(item, 4, at(z, right), high, at(z, left))

    def send_pair(item, slots, rows):
        hop(item, slots[0], at(other, x), rows, at(z, right))
        hop(item, slots[1], at(other, x), rows, at(z, left))

    def send_cross(item):
        landed(item, 3, at(z, far), low)
        hop(item, 9, at(z, far), low, at(other, x))
        landed(item, 4, at(z, far), high)
        hop(item, 10, at(z, far), high, at(other, x))

    send_own(OWN)

    arrived(ids_all, ids_recv)
    ids_copy = pltpu.make_async_copy(ids_all, ids_s, ids_copy_sem)
    ids_copy.start()
    ids_copy.wait()
    arrived(first, first_recv)
    band = lax.rem(lax.broadcasted_iota(jnp.int32, first.shape[1:], 1), bands)

    for item in (PLUS, MINUS):
        def choose(j, carry):
            partner = ids_s[j, 0, item]
            values = first[partner].astype(jnp.float32)
            keep = band < ids_s[partner, 0, 2]
            picked[item, j] = jnp.where(keep, values, jnp.zeros_like(values)).astype(jnp.bfloat16)
            return carry

        lax.fori_loop(0, ka, choose, 0)

        def deliver(step, carry):
            j = lax.rem(k + step, ka)
            to(picked.at[item, j], gath.at[item, p, k], second_send.at[item], second_recv.at[item], (j, p))
            return carry

        pltpu.make_async_copy(picked.at[item, k], gath.at[item, p, k], second_recv.at[item]).start()
        lax.fori_loop(1, ka, deliver, 0)

    send_far(OWN)
    landed(OWN, 0, at(other, x), whole)
    send_pair(OWN, (5, 7), whole)
    landed(OWN, 5, at(other, left), whole)
    hop(OWN, 9, at(other, left), low, at(z, right))
    landed(OWN, 7, at(other, right), whole)
    hop(OWN, 10, at(other, right), high, at(z, left))

    rows = ka * piece
    for item in (PLUS, MINUS):
        arrived(gath.at[item, p], second_recv.at[item])
        send_own(item)
        mine = gath[item, p].reshape(rows, 2 * bands)
        lhs[item, 0] = mine
        lhs[item, 1] = jnp.concatenate([mine[:, bands:], -mine[:, :bands]], axis=1)

    landed(OWN, 3, at(z, far), low)
    landed(OWN, 4, at(z, far), high)
    landed(OWN, 9, at(other, far), low)
    landed(OWN, 10, at(other, far), high)
    coul_copy.wait()

    def apply(block, part, fresh=False):
        pieces = pl.ds(*part)
        columns = part[1] * piece
        start = pl.multiple_of(block * rows + part[0] * piece, columns)
        phi = gath[OWN, block, pieces].reshape(columns, 2 * bands)
        turned = jnp.concatenate([-phi[:, bands:], phi[:, :bands]], axis=1)
        others = [gath[item, block, pieces].reshape(columns, 2 * bands) for item in (PLUS, MINUS)]
        kernels = [cbuf[item, :, pl.ds(start, columns)].astype(jnp.float32) for item in (PLUS, MINUS)]
        total = None
        for side, values in ((0, phi), (1, turned)):
            mixed = sum(
                kernels[item]
                * lax.dot_general(lhs[item, side], others[item], last_dims, preferred_element_type=jnp.float32)
                for item in (PLUS, MINUS)
            )
            upper = mixed.astype(jnp.bfloat16)
            lower = (mixed - upper.astype(jnp.float32)).astype(jnp.bfloat16)
            for term in (upper, lower):
                product = jnp.dot(term, values, preferred_element_type=jnp.float32)
                total = product if total is None else total + product
        out[0] = total if fresh else out[0] + total

    both = (PLUS, MINUS)
    apply(p, whole, fresh=True)
    for item in both:
        send_far(item)
        landed(item, 0, at(other, x), whole)
    for rows_part, slots in ((low, (5, 7)), (high, (6, 8))):
        for item in both:
            send_pair(item, slots, rows_part)
    apply(at(other, x), whole)
    send_cross(PLUS)
    apply(at(z, left), whole)
    send_cross(MINUS)
    apply(at(z, right), whole)
    apply(at(z, far), whole)
    for part, slots in ((low, (5, 7, 9)), (high, (6, 8, 10))):
        for block, slot in zip((at(other, left), at(other, right), at(other, far)), slots):
            for item in both:
                landed(item, slot, block, part)
            apply(block, part)

    arrived(ids_all.at[pl.ds(0, ka - 1)], ids_send)
    arrived(first.at[pl.ds(0, ka - 1)], first_send)
    for item in both:
        arrived(picked.at[item, pl.ds(0, ka - 1)], second_send.at[item])
        for slot in range(11):
            arrived(gath.at[item, 0, pl.ds(*(whole if slot < 3 else low))], gather_send.at[item, slot])
    for slot in (0, 1, 2, 3, 4, 5, 7, 9, 10):
        arrived(gath.at[OWN, 0, pl.ds(*(low if slot in (3, 4, 9, 10) else whole))], gather_send.at[OWN, slot])


def body(ka, pa, orbitals, occupied, plus_partner, minus_partner, coulomb):
    _, rows, channels = orbitals.shape
    piece = rows // ka
    dma = pltpu.SemaphoreType.DMA
    vmem = pl.BlockSpec(memory_space=pltpu.VMEM)
    hbm = pl.BlockSpec(memory_space=pl.ANY)
    summed = pl.pallas_call(
        functools.partial(kernel, ka, pa),
        out_shape=jax.ShapeDtypeStruct((1, rows, channels), jnp.float32),
        in_specs=[hbm] * 5,
        out_specs=vmem,
        scratch_shapes=[
            pltpu.VMEM((3, pa, ka, piece, channels), jnp.bfloat16),
            pltpu.VMEM((ka, piece, channels), jnp.bfloat16),
            pltpu.SMEM((3, 1), jnp.int32),
            pltpu.VMEM((1, channels), jnp.int32),
            pltpu.VMEM((ka, 1, channels), jnp.int32),
            pltpu.SMEM((ka, 1, channels), jnp.int32),
            pltpu.VMEM((2, ka, piece, channels), jnp.bfloat16),
            pltpu.VMEM(coulomb.shape, jnp.bfloat16),
            pltpu.VMEM((2, 2, rows, channels), jnp.bfloat16),
            dma, dma, dma((3,)), dma, dma, dma, dma, dma, dma((2,)), dma((2,)), dma((3, 11)), dma((3, 11)),
        ],
        compiler_params=pltpu.CompilerParams(collective_id=0, has_side_effects=True),
        name="exchange",
    )(orbitals.reshape(1, ka, piece, channels), occupied, plus_partner, minus_partner, coulomb)
    return -summed


def solution(mesh):
    placed = (P("ka", "pa", None), P("ka"), P("ka"), P("ka"), P(None, "pa", None))
    return jax.shard_map(
        functools.partial(body, mesh.shape["ka"], mesh.shape["pa"]),
        mesh=mesh, in_specs=placed, out_specs=P("ka", "pa", None), check_vma=False,
    )
```

```python
import functools
import math

import jax
import jax.numpy as jnp
from jax import lax
from jax.experimental import pallas as pl
from jax.experimental.pallas import tpu as pltpu
from jax.sharding import PartitionSpec as P

MESH = pl.DeviceIdType.MESH
PLUS, MINUS, OWN = 0, 1, 2
SPLIT = 2
last_dims = (((1,), (1,)), ((), ()))


def kernel(
    ka, pa, orb, occ, plus, minus, coul, out,
    gath, first, numbers, ids_row, ids_all, ids_s, picked, cbuf, lhs,
    own_sem, coul_sem, number_sems, ids_copy_sem, ids_send, ids_recv,
    first_send, first_recv, second_send, second_recv, gather_send, gather_recv,
):
    k, p = lax.axis_index("ka"), lax.axis_index("pa")
    xs = pa // 2
    z, x = p // xs, lax.rem(p, xs)
    other = 1 - z
    right, left, far = [lax.rem(x + step, xs) for step in (1, xs - 1, 2)]
    at = lambda plane, column: plane * xs + column
    half = ka // 2
    split = ka * SPLIT // 4
    whole, low, high = (0, ka), (0, half), (half, half)
    bands = out.shape[2] // 2
    piece = first.shape[1]

    barrier = pltpu.get_barrier_semaphore()

    def greet(step, carry):
        pl.semaphore_signal(barrier, inc=1, device_id=(lax.rem(k + step, ka), p), device_id_type=MESH)
        return carry

    lax.fori_loop(1, ka, greet, 0)
    for peer in (at(other, x), at(z, right), at(z, left)):
        pl.semaphore_signal(barrier, inc=1, device_id=(k, peer), device_id_type=MESH)

    own_copy = pltpu.make_async_copy(orb, gath.at[OWN, pl.ds(p, 1)], own_sem)
    own_copy.start()
    number_copies = [
        pltpu.make_async_copy(ref, numbers.at[index], number_sems.at[index])
        for index, ref in enumerate((plus, minus, occ))
    ]
    for copy in number_copies:
        copy.start()
    coul_copy = pltpu.make_async_copy(coul, cbuf, coul_sem)
    coul_copy.start()
    for copy in number_copies:
        copy.wait()
    lane = lax.broadcasted_iota(jnp.int32, (1, 2 * bands), 1)
    ids_row[...] = jnp.where(lane == 0, numbers[0, 0], jnp.where(lane == 1, numbers[1, 0], numbers[2, 0]))
    own_copy.wait()
    pl.semaphore_wait(barrier, ka + 2)

    def to(source, target, send, recv, device):
        pltpu.make_async_remote_copy(
            src_ref=source, dst_ref=target, send_sem=send, recv_sem=recv,
            device_id=device, device_id_type=MESH,
        ).start()

    def arrived(ref, sem):
        pltpu.make_async_copy(ref, ref, sem).wait()

    def tell(step, carry):
        to(ids_row, ids_all.at[k], ids_send, ids_recv, (lax.rem(k + step, ka), p))
        return carry

    def spread(step, carry):
        j = lax.rem(k + step, ka)
        to(gath.at[OWN, p, j], first.at[k], first_send, first_recv, (j, p))
        return carry

    pltpu.make_async_copy(ids_row, ids_all.at[k], ids_recv).start()
    pltpu.make_async_copy(gath.at[OWN, p, k], first.at[k], first_recv).start()
    lax.fori_loop(1, ka, tell, 0)
    lax.fori_loop(1, ka, spread, 0)

    def hop(item, slot, block, rows, peer):
        part = gath.at[item, block, pl.ds(*rows)]
        to(part, part, gather_send.at[item, slot], gather_recv.at[item, slot], (k, peer))

    def landed(item, slot, block, rows):
        arrived(gath.at[item, block, pl.ds(*rows)], gather_recv.at[item, slot])

    def send_own(item):
        hop(item, 1, p, whole, at(z, right))
        hop(item, 2, p, whole, at(z, left))
        hop(item, 0, p, whole, at(other, x))

    def send_far(item):
        landed(item, 1, at(z, left), whole)
        hop(item, 3, at(z, left), low, at(z, right))
        landed(item, 2, at(z, right), whole)
        hop(item, 4, at(z, right), high, at(z, left))

    def send_pair(item, slots, rows):
        hop(item, slots[0], at(other, x), rows, at(z, right))
        hop(item, slots[1], at(other, x), rows, at(z, left))

    def send_cross(item):
        landed(item, 3, at(z, far), low)
        hop(item, 9, at(z, far), low, at(other, x))
        landed(item, 4, at(z, far), high)
        hop(item, 10, at(z, far), high, at(other, x))

    send_own(OWN)

    arrived(ids_all, ids_recv)
    ids_copy = pltpu.make_async_copy(ids_all, ids_s, ids_copy_sem)
    ids_copy.start()
    ids_copy.wait()
    arrived(first, first_recv)
    band = lax.rem(lax.broadcasted_iota(jnp.int32, first.shape[1:], 1), bands)

    for item in (PLUS, MINUS):
        def choose(j, carry):
            partner = ids_s[j, 0, item]
            values = first[partner].astype(jnp.float32)
            keep = band < ids_s[partner, 0, 2]
            picked[item, j] = jnp.where(keep, values, jnp.zeros_like(values)).astype(jnp.bfloat16)
            return carry

        lax.fori_loop(0, ka, choose, 0)

        def deliver(step, carry):
            j = lax.rem(k + step, ka)
            to(picked.at[item, j], gath.at[item, p, k], second_send.at[item], second_recv.at[item], (j, p))
            return carry

        pltpu.make_async_copy(picked.at[item, k], gath.at[item, p, k], second_recv.at[item]).start()
        lax.fori_loop(1, ka, deliver, 0)

    send_far(OWN)
    landed(OWN, 0, at(other, x), whole)
    send_pair(OWN, (5, 7), whole)
    landed(OWN, 5, at(other, left), whole)
    hop(OWN, 9, at(other, left), low, at(z, right))
    landed(OWN, 7, at(other, right), whole)
    hop(OWN, 10, at(other, right), high, at(z, left))

    rows = ka * piece
    for item in (PLUS, MINUS):
        arrived(gath.at[item, p], second_recv.at[item])
        send_own(item)
        mine = gath[item, p].reshape(rows, 2 * bands)
        lhs[item, 0] = mine
        lhs[item, 1] = jnp.concatenate([mine[:, bands:], -mine[:, :bands]], axis=1)

    landed(OWN, 3, at(z, far), low)
    landed(OWN, 4, at(z, far), high)
    landed(OWN, 9, at(other, far), low)
    landed(OWN, 10, at(other, far), high)
    coul_copy.wait()

    def apply(block, part, fresh=False):
        pieces = pl.ds(*part)
        columns = part[1] * piece
        start = pl.multiple_of(block * rows + part[0] * piece, math.gcd(columns, max(part[0] * piece, columns)))
        phi = gath[OWN, block, pieces].reshape(columns, 2 * bands)
        turned = jnp.concatenate([-phi[:, bands:], phi[:, :bands]], axis=1)
        others = [gath[item, block, pieces].reshape(columns, 2 * bands) for item in (PLUS, MINUS)]
        kernels = [cbuf[item, :, pl.ds(start, columns)].astype(jnp.float32) for item in (PLUS, MINUS)]
        total = None
        for side, values in ((0, phi), (1, turned)):
            mixed = sum(
                kernels[item]
                * lax.dot_general(lhs[item, side], others[item], last_dims, preferred_element_type=jnp.float32)
                for item in (PLUS, MINUS)
            )
            upper = mixed.astype(jnp.bfloat16)
            lower = (mixed - upper.astype(jnp.float32)).astype(jnp.bfloat16)
            for term in (upper, lower):
                product = jnp.dot(term, values, preferred_element_type=jnp.float32)
                total = product if total is None else total + product
        out[0] = total if fresh else out[0] + total

    both = (PLUS, MINUS)
    early, late = (0, split), (split, ka - split)
    apply(p, whole, fresh=True)
    send_far(PLUS)
    landed(PLUS, 0, at(other, x), whole)
    send_pair(PLUS, (5, 7), early)
    send_far(MINUS)
    send_pair(PLUS, (6, 8), late)
    apply(at(z, left), whole)
    send_cross(PLUS)
    landed(MINUS, 0, at(other, x), whole)
    send_pair(MINUS, (5, 7), early)
    send_pair(MINUS, (6, 8), late)
    apply(at(z, right), whole)
    send_cross(MINUS)
    apply(at(other, x), whole)
    apply(at(z, far), whole)
    for side, cross, slots in ((early, low, (5, 7, 9)), (late, high, (6, 8, 10))):
        for block, slot, part in zip(
            (at(other, left), at(other, right), at(other, far)), slots, (side, side, cross)
        ):
            for item in both:
                landed(item, slot, block, part)
            apply(block, part)

    arrived(ids_all.at[pl.ds(0, ka - 1)], ids_send)
    arrived(first.at[pl.ds(0, ka - 1)], first_send)
    for item in both:
        arrived(picked.at[item, pl.ds(0, ka - 1)], second_send.at[item])
        for slots, part in (((0, 1, 2), whole), ((3, 4, 9, 10), low), ((5, 7), early), ((6, 8), late)):
            for slot in slots:
                arrived(gath.at[item, 0, pl.ds(*part)], gather_send.at[item, slot])
    for slot in (0, 1, 2, 3, 4, 5, 7, 9, 10):
        arrived(gath.at[OWN, 0, pl.ds(*(low if slot in (3, 4, 9, 10) else whole))], gather_send.at[OWN, slot])


def body(ka, pa, orbitals, occupied, plus_partner, minus_partner, coulomb):
    _, rows, channels = orbitals.shape
    piece = rows // ka
    dma = pltpu.SemaphoreType.DMA
    vmem = pl.BlockSpec(memory_space=pltpu.VMEM)
    hbm = pl.BlockSpec(memory_space=pl.ANY)
    summed = pl.pallas_call(
        functools.partial(kernel, ka, pa),
        out_shape=jax.ShapeDtypeStruct((1, rows, channels), jnp.float32),
        in_specs=[hbm] * 5,
        out_specs=vmem,
        scratch_shapes=[
            pltpu.VMEM((3, pa, ka, piece, channels), jnp.bfloat16),
            pltpu.VMEM((ka, piece, channels), jnp.bfloat16),
            pltpu.SMEM((3, 1), jnp.int32),
            pltpu.VMEM((1, channels), jnp.int32),
            pltpu.VMEM((ka, 1, channels), jnp.int32),
            pltpu.SMEM((ka, 1, channels), jnp.int32),
            pltpu.VMEM((2, ka, piece, channels), jnp.bfloat16),
            pltpu.VMEM(coulomb.shape, jnp.bfloat16),
            pltpu.VMEM((2, 2, rows, channels), jnp.bfloat16),
            dma, dma, dma((3,)), dma, dma, dma, dma, dma, dma((2,)), dma((2,)), dma((3, 11)), dma((3, 11)),
        ],
        compiler_params=pltpu.CompilerParams(collective_id=0, has_side_effects=True, vmem_limit_bytes=48 << 20),
        name="exchange",
    )(orbitals.reshape(1, ka, piece, channels), occupied, plus_partner, minus_partner, coulomb)
    return -summed


def solution(mesh):
    placed = (P("ka", "pa", None), P("ka"), P("ka"), P("ka"), P(None, "pa", None))
    return jax.shard_map(
        functools.partial(body, mesh.shape["ka"], mesh.shape["pa"]),
        mesh=mesh, in_specs=placed, out_specs=P("ka", "pa", None), check_vma=False,
    )
```

```python
import functools

import jax
import jax.numpy as jnp
from jax import lax
from jax.experimental import pallas as pl
from jax.experimental.pallas import tpu as pltpu
from jax.sharding import PartitionSpec as P

MESH = pl.DeviceIdType.MESH
PLUS, MINUS, OWN = 0, 1, 2
last_dims = (((1,), (1,)), ((), ()))


def kernel(
    ka, pa, orb, occ, plus, minus, coul, out,
    gath, first, numbers, ids_row, ids_all, ids_s, picked, cbuf, lhs,
    own_sem, coul_sem, number_sems, ids_copy_sem, ids_send, ids_recv,
    first_send, first_recv, second_send, second_recv, gather_send, gather_recv,
):
    k, p = lax.axis_index("ka"), lax.axis_index("pa")
    xs = pa // 2
    z, x = p // xs, lax.rem(p, xs)
    other = 1 - z
    right, left, far = [lax.rem(x + step, xs) for step in (1, xs - 1, 2)]
    at = lambda plane, column: plane * xs + column
    half = ka // 2
    whole, low, high = (0, ka), (0, half), (half, half)
    bands = out.shape[2] // 2
    piece = first.shape[1]

    barrier = pltpu.get_barrier_semaphore()

    def greet(step, carry):
        pl.semaphore_signal(barrier, inc=1, device_id=(lax.rem(k + step, ka), p), device_id_type=MESH)
        return carry

    lax.fori_loop(1, ka, greet, 0)
    for peer in (at(other, x), at(z, right), at(z, left)):
        pl.semaphore_signal(barrier, inc=1, device_id=(k, peer), device_id_type=MESH)

    own_copy = pltpu.make_async_copy(orb, gath.at[OWN, pl.ds(p, 1)], own_sem)
    own_copy.start()
    number_copies = [
        pltpu.make_async_copy(ref, numbers.at[index], number_sems.at[index])
        for index, ref in enumerate((plus, minus, occ))
    ]
    for copy in number_copies:
        copy.start()
    coul_copy = pltpu.make_async_copy(coul, cbuf, coul_sem)
    coul_copy.start()
    for copy in number_copies:
        copy.wait()
    lane = lax.broadcasted_iota(jnp.int32, (1, 2 * bands), 1)
    ids_row[...] = jnp.where(lane == 0, numbers[0, 0], jnp.where(lane == 1, numbers[1, 0], numbers[2, 0]))
    own_copy.wait()
    pl.semaphore_wait(barrier, ka + 2)

    def to(source, target, send, recv, device):
        pltpu.make_async_remote_copy(
            src_ref=source, dst_ref=target, send_sem=send, recv_sem=recv,
            device_id=device, device_id_type=MESH,
        ).start()

    def arrived(ref, sem):
        pltpu.make_async_copy(ref, ref, sem).wait()

    def tell(step, carry):
        to(ids_row, ids_all.at[k], ids_send, ids_recv, (lax.rem(k + step, ka), p))
        return carry

    def spread(step, carry):
        j = lax.rem(k + step, ka)
        to(gath.at[OWN, p, j], first.at[k], first_send, first_recv, (j, p))
        return carry

    pltpu.make_async_copy(ids_row, ids_all.at[k], ids_recv).start()
    pltpu.make_async_copy(gath.at[OWN, p, k], first.at[k], first_recv).start()
    lax.fori_loop(1, ka, tell, 0)
    lax.fori_loop(1, ka, spread, 0)

    def hop(item, slot, block, rows, peer):
        part = gath.at[item, block, pl.ds(*rows)]
        to(part, part, gather_send.at[item, slot], gather_recv.at[item, slot], (k, peer))

    def landed(item, slot, block, rows):
        arrived(gath.at[item, block, pl.ds(*rows)], gather_recv.at[item, slot])

    def send_own(item, part, slots):
        hop(item, slots[1], p, part, at(z, right))
        hop(item, slots[2], p, part, at(z, left))
        hop(item, slots[0], p, part, at(other, x))

    def send_far(item):
        landed(item, 1, at(z, left), whole)
        hop(item, 3, at(z, left), low, at(z, right))
        landed(item, 2, at(z, right), whole)
        hop(item, 4, at(z, right), high, at(z, left))

    def send_pair(item, slots, rows):
        hop(item, slots[0], at(other, x), rows, at(z, right))
        hop(item, slots[1], at(other, x), rows, at(z, left))

    def cross(item, part, slot):
        landed(item, slot, at(z, far), part)
        hop(item, slot + 6, at(z, far), part, at(other, x))

    send_own(OWN, whole, (0, 1, 2))

    arrived(ids_all, ids_recv)
    ids_copy = pltpu.make_async_copy(ids_all, ids_s, ids_copy_sem)
    ids_copy.start()
    ids_copy.wait()
    arrived(first, first_recv)
    band = lax.rem(lax.broadcasted_iota(jnp.int32, first.shape[1:], 1), bands)

    for item in (PLUS, MINUS):
        def choose(j, carry):
            partner = ids_s[j, 0, item]
            values = first[partner].astype(jnp.float32)
            keep = band < ids_s[partner, 0, 2]
            picked[item, j] = jnp.where(keep, values, jnp.zeros_like(values)).astype(jnp.bfloat16)
            return carry

        lax.fori_loop(0, ka, choose, 0)

        def deliver(step, carry):
            j = lax.rem(k + step, ka)
            to(picked.at[item, j], gath.at[item, p, k], second_send.at[item], second_recv.at[item], (j, p))
            return carry

        pltpu.make_async_copy(picked.at[item, k], gath.at[item, p, k], second_recv.at[item]).start()
        lax.fori_loop(1, ka, deliver, 0)

    send_far(OWN)
    landed(OWN, 0, at(other, x), whole)
    send_pair(OWN, (5, 7), whole)
    landed(OWN, 5, at(other, left), whole)
    hop(OWN, 9, at(other, left), low, at(z, right))
    landed(OWN, 7, at(other, right), whole)
    hop(OWN, 10, at(other, right), high, at(z, left))

    rows = ka * piece
    for item in (PLUS, MINUS):
        arrived(gath.at[item, p], second_recv.at[item])
        if item == PLUS:
            send_own(item, whole, (0, 1, 2))
        else:
            send_own(item, low, (0, 1, 2))
            send_own(item, high, (11, 12, 13))
        mine = gath[item, p].reshape(rows, 2 * bands)
        lhs[item, 0] = mine
        lhs[item, 1] = jnp.concatenate([mine[:, bands:], -mine[:, :bands]], axis=1)

    landed(OWN, 3, at(z, far), low)
    landed(OWN, 4, at(z, far), high)
    landed(OWN, 9, at(other, far), low)
    landed(OWN, 10, at(other, far), high)
    coul_copy.wait()

    def apply(*parts, fresh=False):
        def join(pieces, axis):
            return pieces[0] if len(pieces) == 1 else jnp.concatenate(pieces, axis=axis)

        def points(item):
            return join(
                [gath[item, block, pl.ds(*part)].reshape(part[1] * piece, 2 * bands) for block, part in parts], 0
            )

        def weights(item):
            spans = []
            for block, part in parts:
                columns = part[1] * piece
                start = pl.multiple_of(block * rows + part[0] * piece, columns)
                spans.append(cbuf[item, :, pl.ds(start, columns)])
            return join(spans, 1).astype(jnp.float32)

        phi = points(OWN)
        turned = jnp.concatenate([-phi[:, bands:], phi[:, :bands]], axis=1)
        others = [points(item) for item in (PLUS, MINUS)]
        kernels = [weights(item) for item in (PLUS, MINUS)]
        total = None
        for side, values in ((0, phi), (1, turned)):
            mixed = sum(
                kernels[item]
                * lax.dot_general(lhs[item, side], others[item], last_dims, preferred_element_type=jnp.float32)
                for item in (PLUS, MINUS)
            )
            upper = mixed.astype(jnp.bfloat16)
            lower = (mixed - upper.astype(jnp.float32)).astype(jnp.bfloat16)
            for term in (upper, lower):
                product = jnp.dot(term, values, preferred_element_type=jnp.float32)
                total = product if total is None else total + product
        out[0] = total if fresh else out[0] + total

    both = (PLUS, MINUS)
    apply((p, whole), fresh=True)
    send_far(PLUS)
    landed(PLUS, 0, at(other, x), whole)
    landed(MINUS, 1, at(z, left), low)
    hop(MINUS, 3, at(z, left), low, at(z, right))
    landed(MINUS, 2, at(z, right), low)
    apply((at(z, left), low), (at(z, right), low))
    landed(MINUS, 13, at(z, right), high)
    hop(MINUS, 4, at(z, right), high, at(z, left))
    send_pair(PLUS, (5, 7), low)
    landed(MINUS, 12, at(z, left), high)
    apply((at(z, left), high), (at(z, right), high))
    cross(PLUS, low, 3)
    cross(PLUS, high, 4)
    landed(MINUS, 0, at(other, x), low)
    send_pair(MINUS, (5, 7), low)
    send_pair(PLUS, (6, 8), high)
    landed(MINUS, 11, at(other, x), high)
    send_pair(MINUS, (6, 8), high)
    cross(MINUS, low, 3)
    apply((at(other, x), whole))
    cross(MINUS, high, 4)
    apply((at(z, far), whole))
    for part, slots in ((low, (5, 7, 9)), (high, (6, 8, 10))):
        for item in both:
            landed(item, slots[0], at(other, left), part)
            landed(item, slots[1], at(other, right), part)
        apply((at(other, left), part), (at(other, right), part))
        for item in both:
            landed(item, slots[2], at(other, far), part)
        apply((at(other, far), part))

    arrived(ids_all.at[pl.ds(0, ka - 1)], ids_send)
    arrived(first.at[pl.ds(0, ka - 1)], first_send)
    for item in both:
        arrived(picked.at[item, pl.ds(0, ka - 1)], second_send.at[item])
        for slot in range(11 if item == PLUS else 14):
            large = item == PLUS and slot < 3
            arrived(gath.at[item, 0, pl.ds(*(whole if large else low))], gather_send.at[item, slot])
    for slot in (0, 1, 2, 3, 4, 5, 7, 9, 10):
        arrived(gath.at[OWN, 0, pl.ds(*(low if slot in (3, 4, 9, 10) else whole))], gather_send.at[OWN, slot])


def body(ka, pa, orbitals, occupied, plus_partner, minus_partner, coulomb):
    _, rows, channels = orbitals.shape
    piece = rows // ka
    dma = pltpu.SemaphoreType.DMA
    vmem = pl.BlockSpec(memory_space=pltpu.VMEM)
    hbm = pl.BlockSpec(memory_space=pl.ANY)
    summed = pl.pallas_call(
        functools.partial(kernel, ka, pa),
        out_shape=jax.ShapeDtypeStruct((1, rows, channels), jnp.float32),
        in_specs=[hbm] * 5,
        out_specs=vmem,
        scratch_shapes=[
            pltpu.VMEM((3, pa, ka, piece, channels), jnp.bfloat16),
            pltpu.VMEM((ka, piece, channels), jnp.bfloat16),
            pltpu.SMEM((3, 1), jnp.int32),
            pltpu.VMEM((1, channels), jnp.int32),
            pltpu.VMEM((ka, 1, channels), jnp.int32),
            pltpu.SMEM((ka, 1, channels), jnp.int32),
            pltpu.VMEM((2, ka, piece, channels), jnp.bfloat16),
            pltpu.VMEM(coulomb.shape, jnp.bfloat16),
            pltpu.VMEM((2, 2, rows, channels), jnp.bfloat16),
            dma, dma, dma((3,)), dma, dma, dma, dma, dma, dma((2,)), dma((2,)), dma((3, 14)), dma((3, 14)),
        ],
        compiler_params=pltpu.CompilerParams(collective_id=0, has_side_effects=True, vmem_limit_bytes=48 << 20),
        name="exchange",
    )(orbitals.reshape(1, ka, piece, channels), occupied, plus_partner, minus_partner, coulomb)
    return -summed


def solution(mesh):
    placed = (P("ka", "pa", None), P("ka"), P("ka"), P("ka"), P(None, "pa", None))
    return jax.shard_map(
        functools.partial(body, mesh.shape["ka"], mesh.shape["pa"]),
        mesh=mesh, in_specs=placed, out_specs=P("ka", "pa", None), check_vma=False,
    )
```

```python
import functools

import jax
import jax.numpy as jnp
from jax import lax
from jax.experimental import pallas as pl
from jax.experimental.pallas import tpu as pltpu
from jax.sharding import PartitionSpec as P

MESH = pl.DeviceIdType.MESH
PLUS, MINUS, OWN = 0, 1, 2
last_dims = (((1,), (1,)), ((), ()))


def kernel(
    ka, pa, orb, occ, plus, minus, coul, out,
    gath, first, numbers, ids_row, ids_all, ids_s, picked, cbuf, lhs, ready,
    own_sem, coul_sem, number_sems, ids_copy_sem, ids_send, ids_recv,
    first_send, first_recv, second_send, second_recv, gather_send, gather_recv,
):
    k, p = lax.axis_index("ka"), lax.axis_index("pa")
    xs = pa // 2
    z, x = p // xs, lax.rem(p, xs)
    other = 1 - z
    right, left, far = [lax.rem(x + step, xs) for step in (1, xs - 1, 2)]
    at = lambda plane, column: plane * xs + column
    half = ka // 2
    whole, low, high = (0, ka), (0, half), (half, half)
    bands = out.shape[2] // 2
    piece = first.shape[1]

    barrier = pltpu.get_barrier_semaphore()

    def greet(step, carry):
        pl.semaphore_signal(barrier, inc=1, device_id=(lax.rem(k + step, ka), p), device_id_type=MESH)
        return carry

    lax.fori_loop(1, ka, greet, 0)
    for peer in (at(other, x), at(z, right), at(z, left)):
        pl.semaphore_signal(barrier, inc=1, device_id=(k, peer), device_id_type=MESH)

    own_copy = pltpu.make_async_copy(orb, gath.at[OWN, pl.ds(p, 1)], own_sem)
    own_copy.start()
    number_copies = [
        pltpu.make_async_copy(ref, numbers.at[index], number_sems.at[index])
        for index, ref in enumerate((plus, minus, occ))
    ]
    for copy in number_copies:
        copy.start()
    coul_copy = pltpu.make_async_copy(coul, cbuf, coul_sem)
    coul_copy.start()
    for copy in number_copies:
        copy.wait()
    lane = lax.broadcasted_iota(jnp.int32, (1, 2 * bands), 1)
    ids_row[...] = jnp.where(lane == 0, numbers[0, 0], jnp.where(lane == 1, numbers[1, 0], numbers[2, 0]))
    own_copy.wait()
    pl.semaphore_wait(barrier, ka + 2)

    def to(source, target, send, recv, device):
        pltpu.make_async_remote_copy(
            src_ref=source, dst_ref=target, send_sem=send, recv_sem=recv,
            device_id=device, device_id_type=MESH,
        ).start()

    def arrived(ref, sem):
        pltpu.make_async_copy(ref, ref, sem).wait()

    def tell(step, carry):
        to(ids_row, ids_all.at[k], ids_send, ids_recv, (lax.rem(k + step, ka), p))
        return carry

    def spread(step, carry):
        j = lax.rem(k + step, ka)
        to(gath.at[OWN, p, j], first.at[k], first_send, first_recv, (j, p))
        return carry

    pltpu.make_async_copy(ids_row, ids_all.at[k], ids_recv).start()
    pltpu.make_async_copy(gath.at[OWN, p, k], first.at[k], first_recv).start()
    lax.fori_loop(1, ka, tell, 0)
    lax.fori_loop(1, ka, spread, 0)

    def hop(item, slot, block, rows, peer):
        part = gath.at[item, block, pl.ds(*rows)]
        to(part, part, gather_send.at[item, slot], gather_recv.at[item, slot], (k, peer))

    def landed(item, slot, block, rows):
        arrived(gath.at[item, block, pl.ds(*rows)], gather_recv.at[item, slot])

    def send_own(item, part, slots):
        hop(item, slots[1], p, part, at(z, right))
        hop(item, slots[2], p, part, at(z, left))
        hop(item, slots[0], p, part, at(other, x))

    def send_far(item):
        landed(item, 1, at(z, left), whole)
        hop(item, 3, at(z, left), low, at(z, right))
        landed(item, 2, at(z, right), whole)
        hop(item, 4, at(z, right), high, at(z, left))

    def send_pair(item, slots, rows):
        hop(item, slots[0], at(other, x), rows, at(z, right))
        hop(item, slots[1], at(other, x), rows, at(z, left))

    def cross(item, part, slot):
        landed(item, slot, at(z, far), part)
        hop(item, slot + 6, at(z, far), part, at(other, x))

    send_own(OWN, whole, (0, 1, 2))

    arrived(ids_all, ids_recv)
    ids_copy = pltpu.make_async_copy(ids_all, ids_s, ids_copy_sem)
    ids_copy.start()
    ids_copy.wait()
    arrived(first, first_recv)
    band = lax.rem(lax.broadcasted_iota(jnp.int32, first.shape[1:], 1), bands)

    for item in (PLUS, MINUS):
        def choose(j, carry):
            partner = ids_s[j, 0, item]
            values = first[partner].astype(jnp.float32)
            keep = band < ids_s[partner, 0, 2]
            picked[item, j] = jnp.where(keep, values, jnp.zeros_like(values)).astype(jnp.bfloat16)
            return carry

        lax.fori_loop(0, ka, choose, 0)

        def deliver(step, carry):
            j = lax.rem(k + step, ka)
            to(picked.at[item, j], gath.at[item, p, k], second_send.at[item], second_recv.at[item], (j, p))
            return carry

        pltpu.make_async_copy(picked.at[item, k], gath.at[item, p, k], second_recv.at[item]).start()
        lax.fori_loop(1, ka, deliver, 0)

    send_far(OWN)
    landed(OWN, 0, at(other, x), whole)
    send_pair(OWN, (5, 7), whole)
    landed(OWN, 5, at(other, left), whole)
    hop(OWN, 9, at(other, left), low, at(z, right))
    landed(OWN, 7, at(other, right), whole)
    hop(OWN, 10, at(other, right), high, at(z, left))

    rows = ka * piece
    for item in (PLUS, MINUS):
        arrived(gath.at[item, p], second_recv.at[item])
        if item == PLUS:
            send_own(item, whole, (0, 1, 2))
        else:
            send_own(item, low, (0, 1, 2))
            send_own(item, high, (11, 12, 13))
        mine = gath[item, p].reshape(rows, 2 * bands)
        lhs[item, 0] = mine
        lhs[item, 1] = jnp.concatenate([mine[:, bands:], -mine[:, :bands]], axis=1)

    landed(OWN, 3, at(z, far), low)
    landed(OWN, 4, at(z, far), high)
    landed(OWN, 9, at(other, far), low)
    landed(OWN, 10, at(other, far), high)
    coul_copy.wait()

    def apply(*parts, fresh=False, prime=None, primed=None):
        def join(pieces, axis):
            return pieces[0] if len(pieces) == 1 else jnp.concatenate(pieces, axis=axis)

        def points(item):
            return join(
                [gath[item, block, pl.ds(*part)].reshape(part[1] * piece, 2 * bands) for block, part in parts], 0
            )

        def weights(item):
            spans = []
            for block, part in parts:
                columns = part[1] * piece
                start = pl.multiple_of(block * rows + part[0] * piece, columns)
                spans.append(cbuf[item, :, pl.ds(start, columns)])
            return join(spans, 1).astype(jnp.float32)

        phi = points(OWN)
        turned = jnp.concatenate([-phi[:, bands:], phi[:, :bands]], axis=1)
        others = [points(item) for item in (PLUS, MINUS)]
        kernels = [weights(item) for item in (PLUS, MINUS)]
        total = None
        span = pl.ds(0, sum(part[1] for _, part in parts) * piece)

        def share(item, side):
            return kernels[item] * lax.dot_general(
                lhs[item, side], others[item], last_dims, preferred_element_type=jnp.float32
            )

        if prime is not None:
            for side in (0, 1):
                ready[prime, side, :, span] = share(PLUS, side)
            return
        for side, values in ((0, phi), (1, turned)):
            plus_share = share(PLUS, side) if primed is None else ready[primed, side, :, span]
            mixed = plus_share + share(MINUS, side)
            upper = mixed.astype(jnp.bfloat16)
            lower = (mixed - upper.astype(jnp.float32)).astype(jnp.bfloat16)
            for term in (upper, lower):
                product = jnp.dot(term, values, preferred_element_type=jnp.float32)
                total = product if total is None else total + product
        out[0] = total if fresh else out[0] + total

    both = (PLUS, MINUS)
    apply((p, whole), fresh=True)
    send_far(PLUS)
    apply((at(z, left), low), (at(z, right), low), prime=0)
    landed(PLUS, 0, at(other, x), whole)
    landed(MINUS, 1, at(z, left), low)
    hop(MINUS, 3, at(z, left), low, at(z, right))
    landed(MINUS, 2, at(z, right), low)
    apply((at(z, left), low), (at(z, right), low), primed=0)
    landed(MINUS, 13, at(z, right), high)
    hop(MINUS, 4, at(z, right), high, at(z, left))
    send_pair(PLUS, (5, 7), low)
    landed(MINUS, 12, at(z, left), high)
    apply((at(z, left), high), (at(z, right), high))
    cross(PLUS, low, 3)
    cross(PLUS, high, 4)
    apply((at(other, x), whole), prime=0)
    landed(MINUS, 0, at(other, x), low)
    send_pair(MINUS, (5, 7), low)
    send_pair(PLUS, (6, 8), high)
    landed(MINUS, 11, at(other, x), high)
    send_pair(MINUS, (6, 8), high)
    cross(MINUS, low, 3)
    apply((at(other, x), whole), primed=0)
    cross(MINUS, high, 4)
    apply((at(z, far), whole))
    for part, slots in ((low, (5, 7, 9)), (high, (6, 8, 10))):
        for item in both:
            landed(item, slots[0], at(other, left), part)
            landed(item, slots[1], at(other, right), part)
        apply((at(other, left), part), (at(other, right), part))
        for item in both:
            landed(item, slots[2], at(other, far), part)
        apply((at(other, far), part))

    arrived(ids_all.at[pl.ds(0, ka - 1)], ids_send)
    arrived(first.at[pl.ds(0, ka - 1)], first_send)
    for item in both:
        arrived(picked.at[item, pl.ds(0, ka - 1)], second_send.at[item])
        for slot in range(11 if item == PLUS else 14):
            large = item == PLUS and slot < 3
            arrived(gath.at[item, 0, pl.ds(*(whole if large else low))], gather_send.at[item, slot])
    for slot in (0, 1, 2, 3, 4, 5, 7, 9, 10):
        arrived(gath.at[OWN, 0, pl.ds(*(low if slot in (3, 4, 9, 10) else whole))], gather_send.at[OWN, slot])


def body(ka, pa, orbitals, occupied, plus_partner, minus_partner, coulomb):
    _, rows, channels = orbitals.shape
    piece = rows // ka
    dma = pltpu.SemaphoreType.DMA
    vmem = pl.BlockSpec(memory_space=pltpu.VMEM)
    hbm = pl.BlockSpec(memory_space=pl.ANY)
    summed = pl.pallas_call(
        functools.partial(kernel, ka, pa),
        out_shape=jax.ShapeDtypeStruct((1, rows, channels), jnp.float32),
        in_specs=[hbm] * 5,
        out_specs=vmem,
        scratch_shapes=[
            pltpu.VMEM((3, pa, ka, piece, channels), jnp.bfloat16),
            pltpu.VMEM((ka, piece, channels), jnp.bfloat16),
            pltpu.SMEM((3, 1), jnp.int32),
            pltpu.VMEM((1, channels), jnp.int32),
            pltpu.VMEM((ka, 1, channels), jnp.int32),
            pltpu.SMEM((ka, 1, channels), jnp.int32),
            pltpu.VMEM((2, ka, piece, channels), jnp.bfloat16),
            pltpu.VMEM(coulomb.shape, jnp.bfloat16),
            pltpu.VMEM((2, 2, rows, channels), jnp.bfloat16),
            pltpu.VMEM((2, 2, rows, rows), jnp.float32),
            dma, dma, dma((3,)), dma, dma, dma, dma, dma, dma((2,)), dma((2,)), dma((3, 14)), dma((3, 14)),
        ],
        compiler_params=pltpu.CompilerParams(collective_id=0, has_side_effects=True, vmem_limit_bytes=48 << 20),
        name="exchange",
    )(pltpu.with_memory_space_constraint(orbitals.reshape(1, ka, piece, channels), pltpu.HBM), occupied, plus_partner, minus_partner, coulomb)
    return -summed


def solution(mesh):
    placed = (P("ka", "pa", None), P("ka"), P("ka"), P("ka"), P(None, "pa", None))
    return jax.shard_map(
        functools.partial(body, mesh.shape["ka"], mesh.shape["pa"]),
        mesh=mesh, in_specs=placed, out_specs=P("ka", "pa", None), check_vma=False,
    )
```

```python
import functools

import jax
import jax.numpy as jnp
from jax import lax
from jax.experimental import pallas as pl
from jax.experimental.pallas import tpu as pltpu
from jax.sharding import PartitionSpec as P

MESH = pl.DeviceIdType.MESH
PLUS, MINUS, OWN = 0, 1, 2
last_dims = (((1,), (1,)), ((), ()))


def kernel(
    ka, pa, orb, occ, plus, minus, coul, out,
    gath, first, numbers, ids_row, ids_all, ids_s, picked, cbuf, lhs, ready,
    own_sem, coul_sem, number_sems, ids_copy_sem, ids_send, ids_recv,
    first_send, first_recv, second_send, second_recv, gather_send, gather_recv,
):
    k, p = lax.axis_index("ka"), lax.axis_index("pa")
    xs = pa // 2
    z, x = p // xs, lax.rem(p, xs)
    other = 1 - z
    right, left, far = [lax.rem(x + step, xs) for step in (1, xs - 1, 2)]
    at = lambda plane, column: plane * xs + column
    half = ka // 2
    whole, low, high = (0, ka), (0, half), (half, half)
    bands = out.shape[2] // 2
    piece = first.shape[1]

    barrier = pltpu.get_barrier_semaphore()

    def greet(step, carry):
        pl.semaphore_signal(barrier, inc=1, device_id=(lax.rem(k + step, ka), p), device_id_type=MESH)
        return carry

    lax.fori_loop(1, ka, greet, 0)
    for peer in (at(other, x), at(z, right), at(z, left)):
        pl.semaphore_signal(barrier, inc=1, device_id=(k, peer), device_id_type=MESH)

    own_copy = pltpu.make_async_copy(orb, gath.at[OWN, pl.ds(p, 1)], own_sem)
    own_copy.start()
    number_copies = [
        pltpu.make_async_copy(ref, numbers.at[index], number_sems.at[index])
        for index, ref in enumerate((plus, minus, occ))
    ]
    for copy in number_copies:
        copy.start()
    coul_copy = pltpu.make_async_copy(coul, cbuf, coul_sem)
    coul_copy.start()
    for copy in number_copies:
        copy.wait()
    lane = lax.broadcasted_iota(jnp.int32, (1, 2 * bands), 1)
    ids_row[...] = jnp.where(lane == 0, numbers[0, 0], jnp.where(lane == 1, numbers[1, 0], numbers[2, 0]))
    own_copy.wait()
    pl.semaphore_wait(barrier, ka + 2)

    def to(source, target, send, recv, device):
        pltpu.make_async_remote_copy(
            src_ref=source, dst_ref=target, send_sem=send, recv_sem=recv,
            device_id=device, device_id_type=MESH,
        ).start()

    def arrived(ref, sem):
        pltpu.make_async_copy(ref, ref, sem).wait()

    def tell(step, carry):
        to(ids_row, ids_all.at[k], ids_send, ids_recv, (lax.rem(k + step, ka), p))
        return carry

    def spread(step, carry):
        j = lax.rem(k + step, ka)
        to(gath.at[OWN, p, j], first.at[k], first_send, first_recv, (j, p))
        return carry

    pltpu.make_async_copy(ids_row, ids_all.at[k], ids_recv).start()
    pltpu.make_async_copy(gath.at[OWN, p, k], first.at[k], first_recv).start()
    lax.fori_loop(1, ka, tell, 0)
    lax.fori_loop(1, ka, spread, 0)

    def hop(item, slot, block, rows, peer):
        part = gath.at[item, block, pl.ds(*rows)]
        to(part, part, gather_send.at[item, slot], gather_recv.at[item, slot], (k, peer))

    def landed(item, slot, block, rows):
        arrived(gath.at[item, block, pl.ds(*rows)], gather_recv.at[item, slot])

    def send_own(item, part, slots):
        hop(item, slots[1], p, part, at(z, right))
        hop(item, slots[2], p, part, at(z, left))
        hop(item, slots[0], p, part, at(other, x))

    def send_far(item):
        landed(item, 1, at(z, left), whole)
        hop(item, 3, at(z, left), low, at(z, right))
        landed(item, 2, at(z, right), whole)
        hop(item, 4, at(z, right), high, at(z, left))

    def send_pair(item, slots, rows):
        hop(item, slots[0], at(other, x), rows, at(z, right))
        hop(item, slots[1], at(other, x), rows, at(z, left))

    def cross(item, part, slot):
        landed(item, slot, at(z, far), part)
        hop(item, slot + 6, at(z, far), part, at(other, x))

    send_own(OWN, whole, (0, 1, 2))

    arrived(ids_all, ids_recv)
    ids_copy = pltpu.make_async_copy(ids_all, ids_s, ids_copy_sem)
    ids_copy.start()
    ids_copy.wait()
    arrived(first, first_recv)
    band = lax.rem(lax.broadcasted_iota(jnp.int32, first.shape[1:], 1), bands)

    for item in (PLUS, MINUS):
        def choose(j, carry):
            partner = ids_s[j, 0, item]
            values = first[partner].astype(jnp.float32)
            keep = band < ids_s[partner, 0, 2]
            picked[item, j] = jnp.where(keep, values, jnp.zeros_like(values)).astype(jnp.bfloat16)
            return carry

        lax.fori_loop(0, ka, choose, 0)

        def deliver(step, carry):
            j = lax.rem(k + step, ka)
            to(picked.at[item, j], gath.at[item, p, k], second_send.at[item], second_recv.at[item], (j, p))
            return carry

        pltpu.make_async_copy(picked.at[item, k], gath.at[item, p, k], second_recv.at[item]).start()
        lax.fori_loop(1, ka, deliver, 0)

    send_far(OWN)
    landed(OWN, 0, at(other, x), whole)
    send_pair(OWN, (5, 7), whole)
    landed(OWN, 5, at(other, left), whole)
    hop(OWN, 9, at(other, left), low, at(z, right))
    landed(OWN, 7, at(other, right), whole)
    hop(OWN, 10, at(other, right), high, at(z, left))

    rows = ka * piece
    for item in (PLUS, MINUS):
        arrived(gath.at[item, p], second_recv.at[item])
        if item == PLUS:
            send_own(item, whole, (0, 1, 2))
        else:
            send_own(item, low, (0, 1, 2))
            send_own(item, high, (11, 12, 13))
        mine = gath[item, p].reshape(rows, 2 * bands)
        lhs[item, 0] = mine
        lhs[item, 1] = jnp.concatenate([mine[:, bands:], -mine[:, :bands]], axis=1)

    landed(OWN, 3, at(z, far), low)
    landed(OWN, 4, at(z, far), high)
    landed(OWN, 9, at(other, far), low)
    landed(OWN, 10, at(other, far), high)
    coul_copy.wait()

    def apply(*parts, fresh=False, prime=None, primed=None):
        def join(pieces, axis):
            return pieces[0] if len(pieces) == 1 else jnp.concatenate(pieces, axis=axis)

        def points(item):
            return join(
                [gath[item, block, pl.ds(*part)].reshape(part[1] * piece, 2 * bands) for block, part in parts], 0
            )

        def weights(item):
            spans = []
            for block, part in parts:
                columns = part[1] * piece
                start = pl.multiple_of(block * rows + part[0] * piece, columns)
                spans.append(cbuf[item, :, pl.ds(start, columns)])
            return join(spans, 1).astype(jnp.float32)

        phi = points(OWN)
        turned = jnp.concatenate([-phi[:, bands:], phi[:, :bands]], axis=1)
        others = [points(item) for item in (PLUS, MINUS)]
        kernels = [weights(item) for item in (PLUS, MINUS)]
        total = None
        span = pl.ds(0, sum(part[1] for _, part in parts) * piece)

        def share(item, side):
            return kernels[item] * lax.dot_general(
                lhs[item, side], others[item], last_dims, preferred_element_type=jnp.float32
            )

        if prime is not None:
            for side in (0, 1):
                ready[prime, side, :, span] = share(PLUS, side)
            return
        for side, values in ((0, phi), (1, turned)):
            plus_share = share(PLUS, side) if primed is None else ready[primed, side, :, span]
            mixed = plus_share + share(MINUS, side)
            upper = mixed.astype(jnp.bfloat16)
            lower = (mixed - upper.astype(jnp.float32)).astype(jnp.bfloat16)
            for term in (upper, lower):
                product = jnp.dot(term, values, preferred_element_type=jnp.float32)
                total = product if total is None else total + product
        out[0] = total if fresh else out[0] + total

    both = (PLUS, MINUS)
    apply((p, whole), fresh=True)
    send_far(PLUS)
    apply((at(z, left), low), (at(z, right), low), prime=0)
    landed(PLUS, 0, at(other, x), whole)
    landed(MINUS, 1, at(z, left), low)
    hop(MINUS, 3, at(z, left), low, at(z, right))
    landed(MINUS, 2, at(z, right), low)
    apply((at(z, left), low), (at(z, right), low), primed=0)
    landed(MINUS, 13, at(z, right), high)
    hop(MINUS, 4, at(z, right), high, at(z, left))
    landed(MINUS, 12, at(z, left), high)
    send_pair(PLUS, (5, 7), low)
    apply((at(z, left), high), (at(z, right), high))
    cross(PLUS, low, 3)
    cross(PLUS, high, 4)
    apply((at(other, x), whole), prime=0)
    landed(MINUS, 0, at(other, x), low)
    send_pair(MINUS, (5, 7), low)
    send_pair(PLUS, (6, 8), high)
    landed(MINUS, 11, at(other, x), high)
    send_pair(MINUS, (6, 8), high)
    cross(MINUS, low, 3)
    apply((at(other, x), whole), primed=0)
    cross(MINUS, high, 4)
    apply((at(z, far), whole))
    for part, slots in ((low, (5, 7, 9)), (high, (6, 8, 10))):
        for item in both:
            landed(item, slots[0], at(other, left), part)
            landed(item, slots[1], at(other, right), part)
        apply((at(other, left), part), (at(other, right), part))
        for item in both:
            landed(item, slots[2], at(other, far), part)
        apply((at(other, far), part))

    arrived(ids_all.at[pl.ds(0, ka - 1)], ids_send)
    arrived(first.at[pl.ds(0, ka - 1)], first_send)
    for item in both:
        arrived(picked.at[item, pl.ds(0, ka - 1)], second_send.at[item])
        for slot in range(11 if item == PLUS else 14):
            large = item == PLUS and slot < 3
            arrived(gath.at[item, 0, pl.ds(*(whole if large else low))], gather_send.at[item, slot])
    for slot in (0, 1, 2, 3, 4, 5, 7, 9, 10):
        arrived(gath.at[OWN, 0, pl.ds(*(low if slot in (3, 4, 9, 10) else whole))], gather_send.at[OWN, slot])


def body(ka, pa, orbitals, occupied, plus_partner, minus_partner, coulomb):
    _, rows, channels = orbitals.shape
    piece = rows // ka
    dma = pltpu.SemaphoreType.DMA
    vmem = pl.BlockSpec(memory_space=pltpu.VMEM)
    hbm = pl.BlockSpec(memory_space=pl.ANY)
    summed = pl.pallas_call(
        functools.partial(kernel, ka, pa),
        out_shape=jax.ShapeDtypeStruct((1, rows, channels), jnp.float32),
        in_specs=[hbm] * 5,
        out_specs=vmem,
        scratch_shapes=[
            pltpu.VMEM((3, pa, ka, piece, channels), jnp.bfloat16),
            pltpu.VMEM((ka, piece, channels), jnp.bfloat16),
            pltpu.SMEM((3, 1), jnp.int32),
            pltpu.VMEM((1, channels), jnp.int32),
            pltpu.VMEM((ka, 1, channels), jnp.int32),
            pltpu.SMEM((ka, 1, channels), jnp.int32),
            pltpu.VMEM((2, ka, piece, channels), jnp.bfloat16),
            pltpu.VMEM(coulomb.shape, jnp.bfloat16),
            pltpu.VMEM((2, 2, rows, channels), jnp.bfloat16),
            pltpu.VMEM((2, 2, rows, rows), jnp.float32),
            dma, dma, dma((3,)), dma, dma, dma, dma, dma, dma((2,)), dma((2,)), dma((3, 14)), dma((3, 14)),
        ],
        compiler_params=pltpu.CompilerParams(collective_id=0, has_side_effects=True, vmem_limit_bytes=48 << 20),
        name="exchange",
    )(pltpu.with_memory_space_constraint(orbitals.reshape(1, ka, piece, channels), pltpu.HBM), occupied, plus_partner, minus_partner, coulomb)
    return -summed


def solution(mesh):
    placed = (P("ka", "pa", None), P("ka"), P("ka"), P("ka"), P(None, "pa", None))
    return jax.shard_map(
        functools.partial(body, mesh.shape["ka"], mesh.shape["pa"]),
        mesh=mesh, in_specs=placed, out_specs=P("ka", "pa", None), check_vma=False,
    )
```
